512 devices in a mesh: graph: 64 (over x, z, core), basis: 8 (over y).
Axes of the slice: x: 4, y: 8, z: 8, core: 2. Of those that a mesh axis runs over, the one named last changes fastest.
Arguments:
- edge_feats: bfloat16 [65536, 512], P(('graph', 'basis')), may hold values from -6 to 6
- pre_weight: bfloat16 [512, 512], replicated, may hold values from -0.25 to 0.25
- down_weight: bfloat16 [512, 64], replicated, may hold values from -0.25 to 0.25
- angle_tiles: bfloat16 [1536, 8, 128, 128], P('graph', 'basis'), may hold values from -0.5 to 0.5
- part_source: int32 [1536], P('graph'), may hold values from 0 to 7
- part_owner: int32 [1536, 1], P('graph'), may hold values from 0 to 63; in each aligned block of 24 rows (0 to 23, 24 to 47, ...) at most 2 rows name the same one
- part_target: int32 [1536], P('graph'), may hold values from 0 to 7
- up_weight: bfloat16 [8, 64, 512], P('basis'), may hold values from -0.25 to 0.25
- res_first: bfloat16 [512, 512], replicated, may hold values from -0.25 to 0.25
- res_second: bfloat16 [512, 512], replicated, may hold values from -0.25 to 0.25
- edge_slot: int32 [512, 128], P(('graph', 'basis')), may hold values from 0 to 31, never falling along the last dimension, each value on 1 to 8 neighbouring positions
- slot_owner: int32 [512, 32, 1], P(('graph', 'basis')), may hold values from 0 to 63; in each aligned block of 32 rows (0 to 31, 32 to 63, ..., all dimensions but the last counted through in order) at most 2 rows name the same one
- slot_atom: int32 [512, 32], P(('graph', 'basis')), may hold values from 0 to 31
- atom_feats: bfloat16 [16384, 512], P(('graph', 'basis')), may hold values from -6 to 6
- atom_first: bfloat16 [512, 512], replicated, may hold values from -0.25 to 0.25
- atom_second: bfloat16 [512, 512], replicated, may hold values from -0.25 to 0.25
Outputs:
- edge_update: bfloat16 [65536, 512], P(('graph', 'basis'))
- atom_update: bfloat16 [16384, 512], P(('graph', 'basis'))
The draws below stay inside these ranges and needn't reach their ends.
Inputs may be any that keep to these rules, and one draw needn't show every extreme that they name: `part_owner`: the 24 parts of one graph shard name each shard at most 2 times, a bound that some block reaches. `slot_owner`: the 32 slots of one device name each graph shard at most 2 times, a bound that some block reaches. `edge_slot`: along a device's 128 rows the slot never falls; every slot holds 1 to 8 rows, one exactly 8.
All inputs are finite; a program needn't handle non-finite values.
Results may differ from the reference program's by a relative error of at most 0.015.
Values may be sent and summed in bfloat16 or wider, within the bound.
No kernel may reach another device: no remote copies, remote signals or barrier semaphores. Data moves between devices by JAX's collectives and lax.ppermute only.
A program may use at most 64 MiB of HBM per device.

```python
import math
import jax
import jax.numpy as jnp
import numpy as np
from jax import lax

D = 512
K = 64
D_ATOM = 512
BLOCK = 128
EB_DEV = 8
A_DEV = 32
SEG_MOST = 8
EDGES = 65536
ROWS_DEV = 128
P_DEV = 24
PARTS_SIZE = 1536
CAP = 2
GROUPS = 8
SLOTS = 32
ACAP = 2
ATOMS = 16384
N_GRAPH = 64
N_BASIS = 8


def touch_ends(result, stream_key, smallest, high):
    extent = result.shape
    place = [jax.random.randint(jax.random.fold_in(stream_key, axis), (), 0, extent[axis]) for axis in range(len(extent))]
    result = result.at[tuple(place)].set(smallest)
    longest = extent.index(max(extent))
    place[longest] = (place[longest] + 1) % extent[longest]
    return result.at[tuple(place)].set(high)


def block_scale(rng, dims, shards, smallest, high):
    factor_of, own = 1.0, jax.random.fold_in(rng, 6)
    for axis_at, parts in shards:
        heights = jnp.exp(jax.random.uniform(jax.random.fold_in(own, axis_at), (parts,), jnp.float32, smallest / len(shards), high / len(shards)))
        factor_of = factor_of * jnp.repeat(heights, dims[axis_at] // parts).reshape([-1 if axis == axis_at else 1 for axis in range(len(dims))])
    return factor_of


def length_profile(count, total, bound, lean):
    weights = [(1 << 20) // math.isqrt(standing ** lean) + 1 for standing in range(2, count + 1)]
    spare, given = total - bound - (count - 1), [1] * (count - 1)
    while spare > 0:
        movable = [i for i in range(count - 1) if given[i] < bound]
        mass, remaining = sum([weights[i] for i in movable]), spare
        for i in movable:
            more = min(bound - given[i], max(1, remaining * weights[i] // mass), spare)
            given[i] = given[i] + more
            spare = spare - more
    return np.array([bound] + given)


def uneven(rng, amount, total, most, skew):
    if amount == 2:
        one = jax.random.randint(rng, (), max(1, total - most), min(most, total - 1) + 1)
        return jnp.stack([one, total - one])
    sizes = jnp.asarray(length_profile(amount, total, most, skew), jnp.int32)
    couples = (amount - 1) // 2
    donor, receiver = sizes[1:1 + 2 * couples:2], sizes[2:2 + 2 * couples:2]
    room = jnp.minimum(donor - 1, most - receiver)
    passed = jax.random.randint(jax.random.fold_in(rng, 1), (couples,), 0, 1 << 20) % (room + 1)
    sizes = sizes.at[1:1 + 2 * couples:2].set(donor - passed).at[2:2 + 2 * couples:2].set(receiver + passed)
    return sizes[jax.random.permutation(jax.random.fold_in(rng, 2), amount)]


def shared_out(key, own, number, rows, amount, top, reach, lean):
    ranking = jax.random.permutation(key, amount)
    heavy_load, usual = shares(amount, rows * top, reach, lean, True), shares(amount, rows * top, reach, lean, False)
    places = jnp.arange(amount)

    def named(lengths, rotation):
        used = int((lengths > 0).sum())
        fixed = max(1, used // 4)
        shifted = fixed + (places - fixed + rotation * (used - fixed)) % max(1, amount - fixed)
        return jnp.zeros((amount,), jnp.int32).at[ranking[jnp.where(places < fixed, places, shifted)]].set(jnp.asarray(lengths, jnp.int32))

    lengths = jnp.where(number % 4 == 0, named(heavy_load, number // 4), named(usual, number - number // 4 - 1))
    mixed = jax.random.permutation(jax.random.fold_in(own, 3), amount)
    source_of, sink = mixed[0:amount // 2 * 2:2], mixed[1:amount // 2 * 2:2]
    room = jnp.minimum(lengths[source_of] - 1, reach - lengths[sink]) // 2
    room = jnp.where((source_of == ranking[0]) | (sink == ranking[0]) | (lengths[sink] == 0), 0, jnp.maximum(room, 0))
    shifted = jax.random.randint(jax.random.fold_in(own, 4), (amount // 2,), 0, 1 << 20) % (room + 1)
    lengths = lengths.at[source_of].add(-shifted).at[sink].add(shifted)
    members = jnp.searchsorted(jnp.cumsum(lengths), jnp.arange(rows * top), side="right").astype(jnp.int32)
    listing = members.reshape(top, rows).T
    listing = listing[jax.random.permutation(jax.random.fold_in(own, 1), rows)]
    rotation = jax.random.randint(jax.random.fold_in(own, 2), (rows, 1), 0, top)
    return jnp.take_along_axis(listing, (jnp.arange(top)[None, :] + rotation) % top, axis=1)


def shares(count, total, limit, slope, full):
    loads = [(1 << 20) // math.isqrt(rank ** slope) + 1 for rank in range(1, count + 1)]
    largest = limit if full else min(limit, max(-(-total // count), total * loads[0] // sum(loads)))
    least = 1 if total - largest >= count - 1 else 0
    counts, rest = [largest] + [least] * (count - 1), total - largest - least * (count - 1)
    while rest > 0:
        candidates = [i for i in range(1, count) if counts[i] < largest] or [i for i in range(1, count) if counts[i] < limit]
        pool, remaining = sum([loads[i] for i in candidates]), rest
        for i in candidates:
            addition = min(limit - counts[i], max(1, remaining * loads[i] // pool), rest)
            counts[i] = counts[i] + addition
            rest = rest - addition
    return np.array(counts)


def gaussian(own_key, dims, scale, most, split=(), kind=jnp.bfloat16):
    result = jax.random.normal(own_key, dims, jnp.float32) * scale
    if len(split) > 0:
        result = block_scale(own_key, dims, split, -0.22, 0.18) * result
    return jnp.clip(result, min=-most, max=most).astype(kind)


def setup_inputs(seed: int = 0) -> dict:
    arg_keys = jax.random.split(jax.random.key(seed), 17)
    edge_feats = gaussian(arg_keys[0], (EDGES, D), 1.0, 6.0, ((0, 512),))
    pre_weight = gaussian(arg_keys[1], (D, D), D ** -0.5, 0.25)
    down_weight = gaussian(arg_keys[2], (D, K), D ** -0.5, 0.25)
    angle_tiles = gaussian(arg_keys[3], (PARTS_SIZE, GROUPS, BLOCK, BLOCK), BLOCK ** -0.5, 0.5, ((0, 64), (1, 8)))
    part_source = touch_ends(jax.random.randint(arg_keys[4], (PARTS_SIZE,), 0, EB_DEV), jax.random.fold_in(arg_keys[4], 1), 0, EB_DEV - 1).astype(jnp.int32)
    part_owner_keys = jax.random.split(jax.random.fold_in(arg_keys[5], 1), PARTS_SIZE // P_DEV)
    part_owner_turns = jax.random.permutation(jax.random.fold_in(arg_keys[5], 3), PARTS_SIZE // P_DEV)
    part_owner = jax.vmap(lambda own, number: shared_out(jax.random.fold_in(arg_keys[5], 2), own, number, P_DEV, N_GRAPH, 1, CAP, 2))(part_owner_keys, part_owner_turns).reshape((PARTS_SIZE, 1))
    part_target = touch_ends(jax.random.randint(arg_keys[6], (PARTS_SIZE,), 0, EB_DEV), jax.random.fold_in(arg_keys[6], 1), 0, EB_DEV - 1).astype(jnp.int32)
    up_weight = gaussian(arg_keys[7], (GROUPS, K, D), (N_BASIS * K) ** -0.5, 0.25, ((0, 8),))
    res_first = gaussian(arg_keys[8], (D, D), D ** -0.5, 0.25)
    res_second = gaussian(arg_keys[9], (D, D), D ** -0.5, 0.25)
    edge_slot = jax.vmap(lambda own: jnp.searchsorted(jnp.cumsum(uneven(own, SLOTS, ROWS_DEV, SEG_MOST, 1)), jnp.arange(ROWS_DEV), side="right"))(jax.random.split(arg_keys[10], (N_GRAPH * N_BASIS))).reshape((N_GRAPH * N_BASIS, ROWS_DEV)).astype(jnp.int32)
    slot_owner_keys = jax.random.split(jax.random.fold_in(arg_keys[11], 1), (N_GRAPH * N_BASIS) * SLOTS // SLOTS)
    slot_owner_turns = jax.random.permutation(jax.random.fold_in(arg_keys[11], 3), (N_GRAPH * N_BASIS) * SLOTS // SLOTS)
    slot_owner = jax.vmap(lambda own, number: shared_out(jax.random.fold_in(arg_keys[11], 2), own, number, SLOTS, N_GRAPH, 1, ACAP, 1))(slot_owner_keys, slot_owner_turns).reshape((N_GRAPH * N_BASIS, SLOTS, 1))
    slot_atom = touch_ends(jax.random.randint(arg_keys[12], (N_GRAPH * N_BASIS, SLOTS), 0, A_DEV), jax.random.fold_in(arg_keys[12], 1), 0, A_DEV - 1).astype(jnp.int32)
    atom_feats = gaussian(arg_keys[13], (ATOMS, D_ATOM), 1.0, 6.0, ((0, 512),))
    atom_first = gaussian(arg_keys[14], (D, D_ATOM), D ** -0.5, 0.25)
    atom_second = gaussian(arg_keys[15], (D_ATOM, D_ATOM), D_ATOM ** -0.5, 0.25)
    return {"edge_feats": edge_feats, "pre_weight": pre_weight, "down_weight": down_weight, "angle_tiles": angle_tiles, "part_source": part_source, "part_owner": part_owner, "part_target": part_target, "up_weight": up_weight, "res_first": res_first, "res_second": res_second, "edge_slot": edge_slot, "slot_owner": slot_owner, "slot_atom": slot_atom, "atom_feats": atom_feats, "atom_first": atom_first, "atom_second": atom_second}


def reference(edge_feats, pre_weight, down_weight, angle_tiles, part_source, part_owner, part_target, up_weight, res_first, res_second, edge_slot, slot_owner, slot_atom, atom_feats, atom_first, atom_second):
    projected = jax.nn.silu(jnp.dot(edge_feats, pre_weight, preferred_element_type=jnp.float32)).astype(jnp.bfloat16)
    lowered = jax.nn.silu(jnp.dot(projected, down_weight, preferred_element_type=jnp.float32)).astype(jnp.bfloat16)
    blocks = lowered.reshape(N_GRAPH * EB_DEV, BLOCK, K)
    owner_shard = jnp.arange(PARTS_SIZE, dtype=jnp.int32) // P_DEV
    source_block = (owner_shard * EB_DEV + part_source).astype(jnp.int32)
    target_block = (part_owner[:, 0] * EB_DEV + part_target).astype(jnp.int32)
    sources = blocks[source_block].astype(jnp.float32)

    def per_group(group_tiles):
        product = jnp.einsum("pij,pjk->pik", group_tiles.astype(jnp.float32), sources).astype(jnp.bfloat16)
        summed = jax.ops.segment_sum(product.astype(jnp.float32), target_block, num_segments=N_GRAPH * EB_DEV)
        return summed.reshape(EDGES, K).astype(jnp.bfloat16)

    paired = lax.map(per_group, jnp.moveaxis(angle_tiles, 1, 0))
    columns = jnp.moveaxis(paired, 0, 1).reshape(EDGES, GROUPS * K)
    triplet = jnp.dot(columns, up_weight.reshape(GROUPS * K, D), preferred_element_type=jnp.float32)
    joined = (edge_feats.astype(jnp.float32) + triplet).astype(jnp.bfloat16)
    inner = jax.nn.silu(jnp.dot(joined, res_first, preferred_element_type=jnp.float32)).astype(jnp.bfloat16)
    second = jax.nn.silu(jnp.dot(inner, res_second, preferred_element_type=jnp.float32))
    edge_update = ((joined.astype(jnp.float32) + second) * (0.5 ** 0.5)).astype(jnp.bfloat16)
    device_ids = jnp.arange(N_GRAPH * N_BASIS, dtype=jnp.int32)
    slot_ids = (device_ids[:, None] * SLOTS + edge_slot).reshape(-1).astype(jnp.int32)
    slot_sums = jax.ops.segment_sum(edge_update.astype(jnp.float32), slot_ids, num_segments=N_GRAPH * N_BASIS * SLOTS).astype(jnp.bfloat16)
    atom_ids = (slot_owner[:, :, 0] * N_BASIS + (device_ids % N_BASIS)[:, None]) * A_DEV + slot_atom
    gathered = jax.ops.segment_sum(slot_sums.astype(jnp.float32), atom_ids.reshape(-1).astype(jnp.int32), num_segments=ATOMS).astype(jnp.bfloat16)
    hidden = jax.nn.silu(jnp.dot(gathered, atom_first, preferred_element_type=jnp.float32)).astype(jnp.bfloat16)
    atom_update = (atom_feats.astype(jnp.float32) + jnp.dot(hidden, atom_second, preferred_element_type=jnp.float32)).astype(jnp.bfloat16)
    return edge_update, atom_update
```

```python
import jax
import jax.numpy as jnp
from jax import lax
from jax.experimental import pallas as pl
from jax.experimental.pallas import tpu as pltpu
from jax.sharding import PartitionSpec as P

half_root = 0.5**0.5
f32, bf16, i32 = jnp.float32, jnp.bfloat16, jnp.int32
VMEM = pl.BlockSpec(memory_space=pltpu.VMEM)
SMEM = pl.BlockSpec(memory_space=pltpu.SMEM)
HEAD = 8


def iota(shape, axis):
    return lax.broadcasted_iota(i32, shape, axis)


def silu(v):
    return v / (1.0 + jnp.exp(-v))


def dot(a, b, left, right):
    return lax.dot_general(a, b, (((left,), (right,)), ((), ())), preferred_element_type=f32)


def lower_kernel(edge_ref, pre_ref, down_ref, out_ref):
    projected = silu(dot(edge_ref[...], pre_ref[...], 1, 0)).astype(bf16)
    lowered = silu(dot(down_ref[...], projected, 1, 1)).astype(bf16)
    for i in range(out_ref.shape[0]):
        out_ref[i] = lowered


def column(row):
    n = row.shape[1]
    return jnp.sum(jnp.where(iota((n, n), 0) == iota((n, n), 1), row, 0), axis=1, keepdims=True)


def table_kernel(me_ref, owner_ref, target_ref, slot_ref, slot_owner_ref, slot_atom_ref, head_ref, atoms_ref):
    me = me_ref[0]
    parts = owner_ref.shape[1]
    base = (me % 4) * 32
    slots = slot_owner_ref.shape[1]
    rows = slot_ref.shape[1]
    place = iota((parts, 128), 1) == iota((parts, 128), 0) + base
    owner_row = jnp.sum(jnp.where(place, column(owner_ref[...]), 0), axis=0, keepdims=True)
    target_row = jnp.sum(jnp.where(place, column(target_ref[...]), 0), axis=0, keepdims=True)
    own_row = slot_owner_ref[...]
    own_col = column(own_row)
    same = own_col == own_row
    down, right = iota((slots, slots), 0), iota((slots, slots), 1)
    rank_row = jnp.sum(jnp.where(same & (down < right), 1, 0), axis=0, keepdims=True)
    rank_col = jnp.sum(jnp.where(same & (right < down), 1, 0), axis=1, keepdims=True)
    spot_col = own_col * 2 + rank_col
    spot_row = jnp.sum(
        jnp.where(slot_ref[...] == iota((slots, rows), 0), spot_col, 0), axis=0, keepdims=True
    )
    sub = iota((HEAD, 128), 0)
    head = jnp.where(sub == 0, owner_row, jnp.where(sub == 1, target_row, jnp.where(sub == 2, spot_row, 0)))
    head_ref[...] = head.astype(f32)
    peers = atoms_ref.shape[0]
    atom = slot_atom_ref[...] + 1
    mine = iota((peers, slots), 0) == own_row
    first = jnp.sum(jnp.where(mine & (rank_row == 0), atom, 0), axis=1, keepdims=True)
    second = jnp.sum(jnp.where(mine & (rank_row == 1), atom, 0), axis=1, keepdims=True)
    lane = iota((peers, 128), 1)
    atoms = jnp.where(lane == 2 * me, first, jnp.where(lane == 2 * me + 1, second, 0))
    atoms_ref[...] = atoms.astype(f32)


def product_kernel(source_ref, lowered_ref, tiles_ref, head_ref, atoms_ref, out_ref, scratch):
    parts = tiles_ref.shape[0]
    peers, rows, _ = out_ref.shape
    for p in range(parts):
        product = dot(lowered_ref[source_ref[p]], tiles_ref[p], 1, 1)
        scratch[pl.ds(p, peers, stride=rows), :] = product
    scratch[pl.ds(parts, peers, stride=rows), :] = jnp.broadcast_to(head_ref[0:1, :], (peers, 128))
    scratch[pl.ds(parts + 1, peers, stride=rows), :] = jnp.broadcast_to(head_ref[1:2, :], (peers, 128))
    scratch[pl.ds(parts + 2, peers, stride=rows), :] = atoms_ref[...]
    for r in range(parts + 3, rows):
        scratch[pl.ds(r, peers, stride=rows), :] = jnp.zeros((peers, 128), f32)
    for k in range(peers):
        out_ref[k] = scratch[pl.ds(k * rows, rows), :].astype(bf16)


def combine_kernel(parts, blocks, arrived_ref, out_ref, atoms_ref):
    peers, rows, _ = arrived_ref.shape
    group = 128 // rows
    targets = peers * blocks
    head = arrived_ref[:, parts:rows, :].astype(f32)
    head = jnp.sum(head.reshape(peers // group, group, rows - parts, 128), axis=1)
    atoms_ref[...] = jnp.sum(head, axis=0)
    lane = iota((1, 128), 1)
    valid = (lane % rows) < parts
    row = iota((targets, 128), 0).astype(f32)
    total = jnp.zeros((targets, 128), f32)
    for r in range(0, peers // group, 2):
        hits = []
        for q in (r, r + 1):
            ids = head[q, 1:2, :] * float(peers) + head[q, 0:1, :]
            ids = jnp.where(valid, ids, -1.0)
            hits.append(jnp.where(row == ids, 1.0, 0.0).astype(bf16))
        items = arrived_ref[r * group : (r + 2) * group].reshape(2 * 128, 128)
        total = total + dot(jnp.concatenate(hits, axis=1), items, 1, 0)
    out_ref[...] = total


def edge_kernel(columns_ref, up_ref, edge_ref, first_ref, second_ref, head_ref, out_ref, send_ref, scratch):
    triplet = dot(columns_ref[...].astype(bf16), up_ref[...], 0, 0)
    joined = (edge_ref[...].astype(f32) + triplet).astype(bf16)
    inner = silu(dot(joined, first_ref[...], 1, 0)).astype(bf16)
    second = silu(dot(inner, second_ref[...], 1, 0))
    update = ((joined.astype(f32) + second) * half_root).astype(bf16)
    out_ref[...] = update
    places = send_ref.shape[0] * 2
    chunks = update.shape[1] // 128
    spot = iota((places, update.shape[0]), 0).astype(f32) == head_ref[2:3, :]
    sums = dot(jnp.where(spot, 1.0, 0.0).astype(bf16), update, 1, 0)
    for c in range(chunks):
        scratch[pl.ds(c, places, stride=chunks), :] = sums[:, c * 128 : (c + 1) * 128]
    send_ref[...] = scratch[...].reshape(send_ref.shape).astype(bf16)


def atom_kernel(arrived_ref, ids_ref, feats_ref, first_ref, second_ref, out_ref, scratch):
    places = arrived_ref.shape[0] * 2
    count, width = feats_ref.shape
    chunks = width // 128
    scratch[...] = arrived_ref[...].astype(f32).reshape(scratch.shape)
    hit = (iota((count, places), 0) + 1).astype(f32) == ids_ref[2:3, :]
    hit = jnp.where(hit, 1.0, 0.0).astype(bf16)
    gathered = jnp.concatenate(
        [
            dot(hit, scratch[pl.ds(c, places, stride=chunks), :].astype(bf16), 1, 0)
            for c in range(chunks)
        ],
        axis=1,
    ).astype(bf16)
    hidden = silu(dot(gathered, first_ref[...], 1, 0)).astype(bf16)
    out_ref[...] = (feats_ref[...].astype(f32) + dot(hidden, second_ref[...], 1, 0)).astype(bf16)


def call(kernel, name, specs, outs, *args, scratch=()):
    return pl.pallas_call(
        kernel,
        name=name,
        in_specs=specs,
        out_specs=[VMEM] * len(outs),
        out_shape=[jax.ShapeDtypeStruct(shape, dtype) for shape, dtype in outs],
        scratch_shapes=scratch,
    )(*args)


def body(
    edge_feats,
    pre_weight,
    down_weight,
    angle_tiles,
    part_source,
    part_owner,
    part_target,
    up_weight,
    res_first,
    res_second,
    edge_slot,
    slot_owner,
    slot_atom,
    atom_feats,
    atom_first,
    atom_second,
):
    peers, blocks = lax.axis_size("graph"), lax.axis_size("basis")
    parts = part_source.shape[0]
    narrow = down_weight.shape[1]
    rows, width = edge_feats.shape
    packed = -(-(parts + 3) // 8) * 8
    me = lax.axis_index("graph").astype(i32).reshape(1)

    (lowered,) = call(
        lower_kernel, "lower", [VMEM] * 3, [((blocks, narrow, rows), bf16)],
        edge_feats, pre_weight, down_weight.T,
    )
    lowered = lax.all_to_all(lowered, "basis", 0, 0, tiled=True)
    head, atoms = call(
        table_kernel, "tables", [SMEM] + [VMEM] * 5,
        [((HEAD, 128), f32), ((peers, 128), f32)],
        me, part_owner.reshape(1, parts), part_target.reshape(1, parts), edge_slot,
        slot_owner.reshape(1, -1), slot_atom,
    )
    (send,) = call(
        product_kernel, "products", [SMEM] + [VMEM] * 4, [((peers, packed, 128), bf16)],
        part_source, lowered, angle_tiles.reshape(parts, rows, rows), head, atoms,
        scratch=[pltpu.VMEM((peers * packed, 128), f32)],
    )
    arrived = lax.all_to_all(send, "graph", 0, 0, tiled=True)
    ups = jnp.broadcast_to(up_weight, (blocks, narrow, width))
    ups, _ = lax.optimization_barrier((ups, send))
    ups = lax.all_to_all(ups, "basis", 0, 0, tiled=True)
    summed, ids = call(
        lambda *refs: combine_kernel(parts, blocks, *refs), "combine", [VMEM],
        [((peers * blocks, 128), f32), ((packed - parts, 128), f32)],
        arrived,
    )
    columns = lax.all_to_all(
        summed.reshape(peers * blocks, 1, 128), ("basis", "graph"), 0, 0, tiled=True
    )
    edge_update, send = call(
        edge_kernel, "edges", [VMEM] * 6,
        [((rows, width), bf16), ((peers, 2 * width // 128, 128), bf16)],
        columns.reshape(peers * blocks, 128), ups.reshape(blocks * narrow, width), edge_feats,
        res_first, res_second, head,
        scratch=[pltpu.VMEM((peers * 2 * width // 128, 128), f32)],
    )
    arrived = lax.all_to_all(send, "graph", 0, 0, tiled=True)
    (atom_update,) = call(
        atom_kernel, "atoms", [VMEM] * 5, [(atom_feats.shape, bf16)],
        arrived, ids, atom_feats, atom_first, atom_second,
        scratch=[pltpu.VMEM((peers * 2 * width // 128, 128), f32)],
    )
    return (edge_update, atom_update)


def solution(mesh):
    in_specs = (
        P(("graph", "basis"), None),
        P(),
        P(),
        P("graph", "basis", None, None),
        P("graph"),
        P("graph", None),
        P("graph"),
        P("basis", None, None),
        P(),
        P(),
        P(("graph", "basis"), None),
        P(("graph", "basis"), None, None),
        P(("graph", "basis"), None),
        P(("graph", "basis"), None),
        P(),
        P(),
    )
    out_specs = (P(("graph", "basis"), None), P(("graph", "basis"), None))
    return jax.shard_map(body, mesh=mesh, in_specs=in_specs, out_specs=out_specs, check_vma=False)
```

```python
import jax
import jax.numpy as jnp
from jax import lax
from jax.experimental import pallas as pl
from jax.experimental.pallas import tpu as pltpu
from jax.sharding import PartitionSpec as P

half_root = 0.5**0.5
f32, bf16, i32 = jnp.float32, jnp.bfloat16, jnp.int32
VMEM = pl.BlockSpec(memory_space=pltpu.VMEM)
SMEM = pl.BlockSpec(memory_space=pltpu.SMEM)
HEAD = 8


def iota(shape, axis):
    return lax.broadcasted_iota(i32, shape, axis)


def silu(v):
    return v / (1.0 + jnp.exp(-v))


def dot(a, b, left, right):
    return lax.dot_general(a, b, (((left,), (right,)), ((), ())), preferred_element_type=f32)


def lower_kernel(edge_ref, pre_ref, down_ref, out_ref):
    projected = silu(dot(edge_ref[...], pre_ref[...], 1, 0)).astype(bf16)
    lowered = silu(dot(down_ref[...], projected, 1, 1)).astype(bf16)
    for i in range(out_ref.shape[0]):
        out_ref[i] = lowered


def column(row):
    n = row.shape[1]
    return jnp.sum(jnp.where(iota((n, n), 0) == iota((n, n), 1), row, 0), axis=1, keepdims=True)


def table_kernel(me_ref, owner_ref, target_ref, slot_ref, slot_owner_ref, slot_atom_ref, head_ref, atoms_ref):
    me = me_ref[0]
    parts = owner_ref.shape[1]
    base = (me % 4) * 32
    slots = slot_owner_ref.shape[1]
    rows = slot_ref.shape[1]
    place = iota((parts, 128), 1) == iota((parts, 128), 0) + base
    owner_row = jnp.sum(jnp.where(place, column(owner_ref[...]), 0), axis=0, keepdims=True)
    target_row = jnp.sum(jnp.where(place, column(target_ref[...]), 0), axis=0, keepdims=True)
    own_row = slot_owner_ref[...]
    own_col = column(own_row)
    same = own_col == own_row
    down, right = iota((slots, slots), 0), iota((slots, slots), 1)
    rank_row = jnp.sum(jnp.where(same & (down < right), 1, 0), axis=0, keepdims=True)
    rank_col = jnp.sum(jnp.where(same & (right < down), 1, 0), axis=1, keepdims=True)
    spot_col = own_col * 2 + rank_col
    spot_row = jnp.sum(
        jnp.where(slot_ref[...] == iota((slots, rows), 0), spot_col, 0), axis=0, keepdims=True
    )
    sub = iota((HEAD, 128), 0)
    head = jnp.where(sub == 0, owner_row, jnp.where(sub == 1, target_row, jnp.where(sub == 2, spot_row, 0)))
    head_ref[...] = head.astype(f32)
    peers = atoms_ref.shape[0]
    atom = slot_atom_ref[...] + 1
    mine = iota((peers, slots), 0) == own_row
    first = jnp.sum(jnp.where(mine & (rank_row == 0), atom, 0), axis=1, keepdims=True)
    second = jnp.sum(jnp.where(mine & (rank_row == 1), atom, 0), axis=1, keepdims=True)
    lane = iota((peers, 128), 1)
    atoms = jnp.where(lane == 2 * me, first, jnp.where(lane == 2 * me + 1, second, 0))
    atoms_ref[...] = atoms.astype(f32)


def product_kernel(source_ref, lowered_ref, tiles_ref, head_ref, atoms_ref, out_ref, scratch):
    parts = tiles_ref.shape[0]
    peers, rows, _ = out_ref.shape
    for p in range(parts):
        product = dot(lowered_ref[source_ref[p]], tiles_ref[p], 1, 1)
        scratch[pl.ds(p, peers, stride=rows), :] = product
    scratch[pl.ds(parts, peers, stride=rows), :] = jnp.broadcast_to(head_ref[0:1, :], (peers, 128))
    scratch[pl.ds(parts + 1, peers, stride=rows), :] = jnp.broadcast_to(head_ref[1:2, :], (peers, 128))
    scratch[pl.ds(parts + 2, peers, stride=rows), :] = atoms_ref[...]
    for r in range(parts + 3, rows):
        scratch[pl.ds(r, peers, stride=rows), :] = jnp.zeros((peers, 128), f32)
    for k in range(peers):
        out_ref[k] = scratch[pl.ds(k * rows, rows), :].astype(bf16)


def combine_kernel(parts, blocks, arrived_ref, out_ref, atoms_ref):
    peers, rows, _ = arrived_ref.shape
    group = 128 // rows
    targets = peers * blocks
    head = arrived_ref[:, parts:rows, :].astype(f32)
    head = jnp.sum(head.reshape(peers // group, group, rows - parts, 128), axis=1)
    atoms_ref[...] = jnp.sum(head, axis=0)
    lane = iota((1, 128), 1)
    valid = (lane % rows) < parts
    row = iota((targets, 128), 0).astype(f32)
    total = jnp.zeros((targets, 128), f32)
    for r in range(0, peers // group, 2):
        hits = []
        for q in (r, r + 1):
            ids = head[q, 1:2, :] * float(peers) + head[q, 0:1, :]
            ids = jnp.where(valid, ids, -1.0)
            hits.append(jnp.where(row == ids, 1.0, 0.0).astype(bf16))
        items = arrived_ref[r * group : (r + 2) * group].reshape(2 * 128, 128)
        total = total + dot(jnp.concatenate(hits, axis=1), items, 1, 0)
    out_ref[...] = total


def edge_kernel(
    peers, at_ref, columns_ref, up_ref, swapped_ref, edge_ref, first_ref, second_ref, head_ref, out_ref, send_ref, scratch
):
    core, group = at_ref[0], at_ref[1]
    blocks = columns_ref.shape[0] // peers
    half = up_ref.shape[0] // blocks
    triplet = jnp.zeros(out_ref.shape, f32)
    for side, ref in ((core, up_ref), (1 - core, swapped_ref)):
        found = [
            columns_ref[pl.ds(pl.multiple_of(((group ^ j) * 2 + side) * half, half), half), :]
            for j in range(blocks)
        ]
        triplet = triplet + dot(jnp.concatenate(found, axis=0).astype(bf16), ref[...], 0, 0)
    joined = (edge_ref[...].astype(f32) + triplet).astype(bf16)
    inner = silu(dot(joined, first_ref[...], 1, 0)).astype(bf16)
    second = silu(dot(inner, second_ref[...], 1, 0))
    update = ((joined.astype(f32) + second) * half_root).astype(bf16)
    out_ref[...] = update
    places = send_ref.shape[0] * 2
    chunks = update.shape[1] // 128
    spot = iota((places, update.shape[0]), 0).astype(f32) == head_ref[2:3, :]
    sums = dot(jnp.where(spot, 1.0, 0.0).astype(bf16), update, 1, 0)
    for c in range(chunks):
        scratch[pl.ds(c, places, stride=chunks), :] = sums[:, c * 128 : (c + 1) * 128]
    send_ref[...] = scratch[...].reshape(send_ref.shape).astype(bf16)


def atom_kernel(arrived_ref, ids_ref, feats_ref, first_ref, second_ref, out_ref, scratch):
    places = arrived_ref.shape[0] * 2
    count, width = feats_ref.shape
    chunks = width // 128
    scratch[...] = arrived_ref[...].astype(f32).reshape(scratch.shape)
    hit = (iota((count, places), 0) + 1).astype(f32) == ids_ref[2:3, :]
    hit = jnp.where(hit, 1.0, 0.0).astype(bf16)
    gathered = jnp.concatenate(
        [
            dot(hit, scratch[pl.ds(c, places, stride=chunks), :].astype(bf16), 1, 0)
            for c in range(chunks)
        ],
        axis=1,
    ).astype(bf16)
    hidden = silu(dot(gathered, first_ref[...], 1, 0)).astype(bf16)
    out_ref[...] = (feats_ref[...].astype(f32) + dot(hidden, second_ref[...], 1, 0)).astype(bf16)


def call(kernel, name, specs, outs, *args, scratch=(), keep=(), pinned=True):
    args = [
        pltpu.with_memory_space_constraint(a, pltpu.VMEM) if pinned and s is VMEM else a
        for a, s in zip(args, specs)
    ]
    return pl.pallas_call(
        kernel,
        name=name,
        in_specs=specs,
        out_specs=[VMEM] * len(outs),
        out_shape=[
            jax.ShapeDtypeStruct(shape, dtype) if i in keep else pltpu.VMEM(shape, dtype)
            for i, (shape, dtype) in enumerate(outs)
        ],
        scratch_shapes=scratch,
        compiler_params=pltpu.CompilerParams(vmem_limit_bytes=16 << 20),
    )(*args)


def body(
    edge_feats,
    pre_weight,
    down_weight,
    angle_tiles,
    part_source,
    part_owner,
    part_target,
    up_weight,
    res_first,
    res_second,
    edge_slot,
    slot_owner,
    slot_atom,
    atom_feats,
    atom_first,
    atom_second,
):
    peers, blocks = lax.axis_size("graph"), lax.axis_size("basis")
    parts = part_source.shape[0]
    narrow = down_weight.shape[1]
    rows, width = edge_feats.shape
    packed = -(-(parts + 3) // 8) * 8
    me = lax.axis_index("graph").astype(i32).reshape(1)

    (lowered,) = call(
        lower_kernel, "lower", [VMEM] * 3, [((blocks, narrow, rows), bf16)],
        edge_feats, pre_weight, down_weight.T, pinned=False,
    )
    lowered = lax.all_to_all(lowered, "basis", 0, 0, tiled=True)
    head, atoms = call(
        table_kernel, "tables", [SMEM] + [VMEM] * 5,
        [((HEAD, 128), f32), ((peers, 128), f32)],
        me, part_owner.reshape(1, parts), part_target.reshape(1, parts), edge_slot,
        slot_owner.reshape(1, -1), slot_atom,
    )
    (send,) = call(
        product_kernel, "products", [SMEM] + [VMEM] * 4, [((peers, packed, 128), bf16)],
        part_source, lowered, angle_tiles.reshape(parts, rows, rows), head, atoms,
        scratch=[pltpu.VMEM((peers * packed, 128), f32)],
    )
    arrived = lax.all_to_all(send, "graph", 0, 0, tiled=True)
    core = lax.axis_index("graph") % 2
    half = narrow // 2
    ups = lax.dynamic_slice_in_dim(up_weight[0], core * half, half, 0)
    ups, _ = lax.optimization_barrier((ups, lowered))
    step = 1
    while step < blocks:
        other = lax.ppermute(ups, "basis", [(j, j ^ step) for j in range(blocks)])
        ups = jnp.concatenate([ups, other], axis=0)
        step *= 2
    swapped = lax.ppermute(ups, "graph", [(j, j ^ 1) for j in range(peers)])
    summed, ids = call(
        lambda *refs: combine_kernel(parts, blocks, *refs), "combine", [VMEM],
        [((peers * blocks, 128), f32), ((packed - parts, 128), f32)],
        arrived,
    )
    columns = lax.all_to_all(
        summed.reshape(peers * blocks, 1, 128), ("basis", "graph"), 0, 0, tiled=True
    )
    edge_update, send = call(
        lambda *refs: edge_kernel(peers, *refs), "edges", [SMEM] + [VMEM] * 7,
        [((rows, width), bf16), ((peers, 2 * width // 128, 128), bf16)],
        jnp.stack([core, lax.axis_index("basis")]).astype(i32),
        columns.reshape(peers * blocks, 128), ups, swapped, edge_feats,
        res_first, res_second, head, keep=(0,),
        scratch=[pltpu.VMEM((peers * 2 * width // 128, 128), f32)],
    )
    arrived = lax.all_to_all(send, "graph", 0, 0, tiled=True)
    (atom_update,) = call(
        atom_kernel, "atoms", [VMEM] * 5, [(atom_feats.shape, bf16)],
        arrived, ids, atom_feats, atom_first, atom_second, keep=(0,),
        scratch=[pltpu.VMEM((peers * 2 * width // 128, 128), f32)],
    )
    return (edge_update, atom_update)


def solution(mesh):
    in_specs = (
        P(("graph", "basis"), None),
        P(),
        P(),
        P("graph", "basis", None, None),
        P("graph"),
        P("graph", None),
        P("graph"),
        P("basis", None, None),
        P(),
        P(),
        P(("graph", "basis"), None),
        P(("graph", "basis"), None, None),
        P(("graph", "basis"), None),
        P(("graph", "basis"), None),
        P(),
        P(),
    )
    out_specs = (P(("graph", "basis"), None), P(("graph", "basis"), None))
    return jax.shard_map(body, mesh=mesh, in_specs=in_specs, out_specs=out_specs, check_vma=False)
```

```python
import jax
import jax.numpy as jnp
from jax import lax
from jax.experimental import pallas as pl
from jax.experimental.pallas import tpu as pltpu
from jax.sharding import PartitionSpec as P

half_root = 0.5**0.5
f32, bf16, i32 = jnp.float32, jnp.bfloat16, jnp.int32
VMEM = pl.BlockSpec(memory_space=pltpu.VMEM)
SMEM = pl.BlockSpec(memory_space=pltpu.SMEM)
GRAPH = ("x", "z", "core")
HEAD = 8
OFFSET = 256


def iota(shape, axis):
    return lax.broadcasted_iota(i32, shape, axis)


def silu(v):
    return v / (1.0 + jnp.exp(-v))


def dot(a, b, left, right):
    return lax.dot_general(a, b, (((left,), (right,)), ((), ())), preferred_element_type=f32)


def lower_kernel(z_size, edge_ref, pre_ref, down_ref, out_ref):
    projected = silu(dot(edge_ref[...], pre_ref[...], 1, 0)).astype(bf16)
    lowered = silu(dot(down_ref[...], projected, 1, 1)).astype(bf16)
    narrow = lowered.shape[0]
    to, at = iota((narrow, narrow), 0), iota((narrow, narrow), 1)
    feature = (to // 2 % z_size) * (narrow // z_size) + to // (2 * z_size) * 2 + to % 2
    order = jnp.where(at == feature, 1.0, 0.0).astype(bf16)
    lowered = dot(order, lowered, 1, 0).astype(bf16)
    for i in range(out_ref.shape[0]):
        out_ref[i] = lowered


def column(row):
    n = row.shape[1]
    return jnp.sum(jnp.where(iota((n, n), 0) == iota((n, n), 1), row, 0), axis=1, keepdims=True)


def table_kernel(sizes, me_ref, owner_ref, target_ref, slot_ref, slot_owner_ref, slot_atom_ref, head_ref, atoms_ref):
    me = me_ref[0]
    parts = owner_ref.shape[1]
    slots = slot_owner_ref.shape[1]
    rows = slot_ref.shape[1]
    owner = column(owner_ref[...])
    z_size, blocks = sizes
    x, z, core = owner // (2 * z_size), (owner // 2) % z_size, owner % 2
    ids = ((x * 2 + core) * blocks + column(target_ref[...])) * z_size + z - OFFSET
    place = iota((parts, 128), 1) == (iota((parts, 128), 0) + me * (parts + 2)) % 128
    id_row = jnp.sum(jnp.where(place, ids, 0), axis=0, keepdims=True)
    own_row = slot_owner_ref[...]
    own_col = column(own_row)
    same = own_col == own_row
    down, right = iota((slots, slots), 0), iota((slots, slots), 1)
    rank_row = jnp.sum(jnp.where(same & (down < right), 1, 0), axis=0, keepdims=True)
    rank_col = jnp.sum(jnp.where(same & (right < down), 1, 0), axis=1, keepdims=True)
    spot_col = own_col * 2 + rank_col
    spot_row = jnp.sum(
        jnp.where(slot_ref[...] == iota((slots, rows), 0), spot_col, 0), axis=0, keepdims=True
    )
    sub = iota((HEAD, 128), 0)
    head_ref[...] = jnp.where(sub == 0, id_row, jnp.where(sub == 1, spot_row, 0)).astype(f32)
    peers = atoms_ref.shape[0]
    atom = slot_atom_ref[...] + 1
    mine = iota((peers, slots), 0) == own_row
    first = jnp.sum(jnp.where(mine & (rank_row == 0), atom, 0), axis=1, keepdims=True)
    second = jnp.sum(jnp.where(mine & (rank_row == 1), atom, 0), axis=1, keepdims=True)
    lane = iota((peers, 128), 1)
    atoms = jnp.where(lane == 2 * me, first, jnp.where(lane == 2 * me + 1, second, 0))
    atoms_ref[...] = atoms.astype(f32)


def product_kernel(source_ref, lowered_ref, tiles_ref, head_ref, atoms_ref, out_ref, scratch):
    parts = tiles_ref.shape[0]
    peers = atoms_ref.shape[0]
    rows = parts + 2
    for p in range(parts):
        product = dot(lowered_ref[source_ref[p]], tiles_ref[p], 1, 1)
        scratch[pl.ds(p, peers, stride=rows), :] = product
    scratch[pl.ds(parts, peers, stride=rows), :] = jnp.broadcast_to(head_ref[0:1, :], (peers, 128))
    scratch[pl.ds(parts + 1, peers, stride=rows), :] = atoms_ref[...]
    out_ref[...] = scratch[...].astype(bf16)


def combine_kernel(parts, peers, arrived_ref, out_ref, atoms_ref, scratch):
    rows = parts + 2
    targets = out_ref.shape[0]
    scratch[...] = arrived_ref[...].astype(f32)
    heads = scratch[pl.ds(parts, peers, stride=rows), :]
    atoms = jnp.sum(scratch[pl.ds(parts + 1, peers, stride=rows), :], axis=0, keepdims=True)
    atoms_ref[...] = jnp.broadcast_to(atoms, atoms_ref.shape)
    source = iota((peers, 128), 0)
    row = iota((targets, 128), 0).astype(f32)
    chunks = peers * rows // 128
    total = jnp.zeros((targets, 128), f32)
    for r in range(0, chunks, 2):
        hits = []
        for q in range(r, min(r + 2, chunks)):
            item = iota((1, 128), 1) + q * 128
            ids = jnp.sum(jnp.where(source == item // rows, heads, 0.0), axis=0, keepdims=True)
            ids = jnp.where(item % rows < parts, ids + float(OFFSET), -1.0)
            hits.append(jnp.where(row == ids, 1.0, 0.0).astype(bf16))
        items = arrived_ref[r * 128 : (r + len(hits)) * 128, :]
        total = total + dot(jnp.concatenate(hits, axis=1), items, 1, 0)
    out_ref[...] = total.astype(bf16)


def edge_kernel(
    peers, at_ref, columns_ref, up_ref, swapped_ref, edge_ref, first_ref, second_ref, head_ref, out_ref, send_ref, scratch
):
    core, group = at_ref[0], at_ref[1]
    blocks = columns_ref.shape[0] // peers
    half = up_ref.shape[0] // blocks
    triplet = jnp.zeros(out_ref.shape, f32)
    for side, ref in ((core, up_ref), (1 - core, swapped_ref)):
        found = [
            columns_ref[pl.ds(pl.multiple_of(((group ^ j) * 2 + side) * half, half), half), :]
            for j in range(blocks)
        ]
        triplet = triplet + dot(jnp.concatenate(found, axis=0).astype(bf16), ref[...], 0, 0)
    joined = (edge_ref[...].astype(f32) + triplet).astype(bf16)
    inner = silu(dot(joined, first_ref[...], 1, 0)).astype(bf16)
    second = silu(dot(inner, second_ref[...], 1, 0))
    update = ((joined.astype(f32) + second) * half_root).astype(bf16)
    out_ref[...] = update
    places = send_ref.shape[0] * 2
    chunks = update.shape[1] // 128
    spot = iota((places, update.shape[0]), 0).astype(f32) == head_ref[1:2, :]
    sums = dot(jnp.where(spot, 1.0, 0.0).astype(bf16), update, 1, 0)
    for c in range(chunks):
        scratch[pl.ds(c, places, stride=chunks), :] = sums[:, c * 128 : (c + 1) * 128]
    send_ref[...] = scratch[...].reshape(send_ref.shape).astype(bf16)


def atom_kernel(arrived_ref, ids_ref, feats_ref, first_ref, second_ref, out_ref, scratch):
    places = arrived_ref.shape[0] * 2
    count, width = feats_ref.shape
    chunks = width // 128
    scratch[...] = arrived_ref[...].astype(f32).reshape(scratch.shape)
    hit = (iota((count, places), 0) + 1).astype(f32) == ids_ref[0:1, :]
    hit = jnp.where(hit, 1.0, 0.0).astype(bf16)
    gathered = jnp.concatenate(
        [
            dot(hit, scratch[pl.ds(c, places, stride=chunks), :].astype(bf16), 1, 0)
            for c in range(chunks)
        ],
        axis=1,
    ).astype(bf16)
    hidden = silu(dot(gathered, first_ref[...], 1, 0)).astype(bf16)
    out_ref[...] = (feats_ref[...].astype(f32) + dot(hidden, second_ref[...], 1, 0)).astype(bf16)


def call(kernel, name, specs, outs, *args, scratch=(), keep=(), space=pltpu.VMEM):
    args = [
        pltpu.with_memory_space_constraint(a, space) if s is VMEM else a
        for a, s in zip(args, specs)
    ]
    return pl.pallas_call(
        kernel,
        name=name,
        in_specs=specs,
        out_specs=[VMEM] * len(outs),
        out_shape=[
            jax.ShapeDtypeStruct(shape, dtype) if i in keep else pltpu.VMEM(shape, dtype)
            for i, (shape, dtype) in enumerate(outs)
        ],
        scratch_shapes=scratch,
        compiler_params=pltpu.CompilerParams(vmem_limit_bytes=16 << 20),
    )(*args)


def body(
    edge_feats,
    pre_weight,
    down_weight,
    angle_tiles,
    part_source,
    part_owner,
    part_target,
    up_weight,
    res_first,
    res_second,
    edge_slot,
    slot_owner,
    slot_atom,
    atom_feats,
    atom_first,
    atom_second,
):
    z_size, blocks = lax.axis_size("z"), lax.axis_size("basis")
    peers = lax.axis_size(GRAPH)
    parts = part_source.shape[0]
    narrow = down_weight.shape[1]
    rows, width = edge_feats.shape
    packed = parts + 2
    near = peers // z_size
    me = lax.axis_index(GRAPH).astype(i32).reshape(1)
    core, group = lax.axis_index("core"), lax.axis_index("basis")
    half = narrow // 2

    (lowered,) = call(
        lambda *refs: lower_kernel(z_size, *refs), "lower", [VMEM] * 3, [((blocks, narrow, rows), bf16)],
        edge_feats, pre_weight, down_weight.T, space=pltpu.HBM,
    )
    lowered, ups = lax.optimization_barrier((lowered, up_weight))
    ups = lax.dynamic_slice_in_dim(ups[0], core * half, half, 0)
    lowered = lax.all_to_all(lowered, "basis", 0, 0, tiled=True)
    other = lax.ppermute(ups, "basis", [(j, j ^ 1) for j in range(blocks)])
    lowered, other = lax.optimization_barrier((lowered, other))
    head, atoms = call(
        lambda *refs: table_kernel((z_size, blocks), *refs), "tables", [SMEM] + [VMEM] * 5,
        [((HEAD, 128), f32), ((peers, 128), f32)],
        me, part_owner.reshape(1, parts), part_target.reshape(1, parts), edge_slot,
        slot_owner.reshape(1, -1), slot_atom,
    )
    source = jnp.clip(part_source, 0, blocks - 1)
    (send,) = call(
        product_kernel, "products", [SMEM] + [VMEM] * 4, [((peers * packed, 128), bf16)],
        source, lowered, angle_tiles.reshape(parts, rows, rows), head, atoms,
        scratch=[pltpu.VMEM((peers * packed, 128), f32)],
    )
    arrived = lax.all_to_all(send.reshape(peers, packed // 2, 2, 128), GRAPH, 0, 0, tiled=True)
    ups = jnp.concatenate([ups, other], axis=0)
    step = 2
    while step < blocks:
        other = lax.ppermute(ups, "basis", [(j, j ^ step) for j in range(blocks)])
        ups = jnp.concatenate([ups, other], axis=0)
        step *= 2
    swapped = lax.ppermute(ups, "core", [(0, 1), (1, 0)])
    summed, ids = call(
        lambda *refs: combine_kernel(parts, peers, *refs), "combine", [VMEM],
        [((peers * blocks, 128), bf16), ((HEAD, 128), f32)],
        arrived.reshape(peers * packed, 128),
        scratch=[pltpu.VMEM((peers * packed, 128), f32)],
    )
    far = blocks * z_size
    columns = lax.all_to_all(summed.reshape(near, far, 128), ("x", "core"), 0, 0, tiled=True)
    columns = jnp.swapaxes(columns, 0, 1)
    columns = lax.all_to_all(columns, ("basis", "z"), 0, 0, tiled=True)
    edge_update, send = call(
        lambda *refs: edge_kernel(peers, *refs), "edges", [SMEM] + [VMEM] * 7,
        [((rows, width), bf16), ((peers, 2 * width // 128, 128), bf16)],
        jnp.stack([core, group]).astype(i32),
        columns.reshape(peers * blocks, 128), ups, swapped, edge_feats,
        res_first, res_second, head, keep=(0,),
        scratch=[pltpu.VMEM((peers * 2 * width // 128, 128), f32)],
    )
    arrived = lax.all_to_all(send, GRAPH, 0, 0, tiled=True)
    (atom_update,) = call(
        atom_kernel, "atoms", [VMEM] * 5, [(atom_feats.shape, bf16)],
        arrived, ids, atom_feats, atom_first, atom_second, keep=(0,),
        scratch=[pltpu.VMEM((peers * 2 * width // 128, 128), f32)],
    )
    return (edge_update, atom_update)


def solution(mesh):
    shape = (mesh.shape["graph"] // 16, 8, 2, mesh.shape["basis"])
    grid = jax.sharding.Mesh(mesh.devices.reshape(shape), GRAPH + ("basis",))
    both = GRAPH + ("basis",)
    in_specs = (
        P(both, None),
        P(),
        P(),
        P(GRAPH, "basis", None, None),
        P(GRAPH),
        P(GRAPH, None),
        P(GRAPH),
        P("basis", None, None),
        P(),
        P(),
        P(both, None),
        P(both, None, None),
        P(both, None),
        P(both, None),
        P(),
        P(),
    )
    out_specs = (P(both, None), P(both, None))
    return jax.shard_map(body, mesh=grid, in_specs=in_specs, out_specs=out_specs, check_vma=False)
```

```python
import jax
import jax.numpy as jnp
from jax import lax
from jax.experimental import pallas as pl
from jax.experimental.pallas import tpu as pltpu
from jax.sharding import PartitionSpec as P

half_root = 0.5**0.5
f32, bf16, i32 = jnp.float32, jnp.bfloat16, jnp.int32
VMEM = pl.BlockSpec(memory_space=pltpu.VMEM)
SMEM = pl.BlockSpec(memory_space=pltpu.SMEM)
GRAPH = ("x", "z", "core")
STEPS = (4, 2, 1)
ORDER = (0, 4, 2, 6)
HEAD = 8
OFFSET = 256


def iota(shape, axis):
    return lax.broadcasted_iota(i32, shape, axis)


def silu(v):
    return v / (1.0 + jnp.exp(-v))


def dot(a, b, left, right):
    return lax.dot_general(a, b, (((left,), (right,)), ((), ())), preferred_element_type=f32)


def lower_kernel(
    sizes, me_ref, edge_ref, pre_ref, down_ref, source_ref, owner_ref, target_ref, slot_ref, slot_owner_ref,
    slot_atom_ref, out_ref, head_ref, atoms_ref, sources_ref,
):
    z_size = sizes[0]
    sources_ref[...] = source_ref[...]
    tables(sizes, me_ref, owner_ref, target_ref, slot_ref, slot_owner_ref, slot_atom_ref, head_ref, atoms_ref)
    projected = silu(dot(edge_ref[...], pre_ref[...], 1, 0)).astype(bf16)
    lowered = silu(dot(down_ref[...], projected, 1, 1)).astype(bf16)
    narrow = lowered.shape[0]
    to, at = iota((narrow, narrow), 0), iota((narrow, narrow), 1)
    feature = (to // 2 % z_size) * (narrow // z_size) + to // (2 * z_size) * 2 + to % 2
    order = jnp.where(at == feature, 1.0, 0.0).astype(bf16)
    lowered = dot(order, lowered, 1, 0).astype(bf16)
    for i in range(out_ref.shape[0]):
        out_ref[i] = lowered


def column(row):
    n = row.shape[1]
    return jnp.sum(jnp.where(iota((n, n), 0) == iota((n, n), 1), row, 0), axis=1, keepdims=True)


def tables(sizes, me_ref, owner_ref, target_ref, slot_ref, slot_owner_ref, slot_atom_ref, head_ref, atoms_ref):
    me = me_ref[0]
    parts = owner_ref.shape[1]
    slots = slot_owner_ref.shape[1]
    rows = slot_ref.shape[1]
    owner = column(owner_ref[...])
    z_size, blocks = sizes
    x, z, core = owner // (2 * z_size), (owner // 2) % z_size, owner % 2
    ids = ((x * 2 + core) * blocks + column(target_ref[...])) * z_size + z - OFFSET
    place = iota((parts, 128), 1) == (iota((parts, 128), 0) + me * (parts + 2)) % 128
    id_row = jnp.sum(jnp.where(place, ids, 0), axis=0, keepdims=True)
    own_row = slot_owner_ref[...]
    own_col = column(own_row)
    same = own_col == own_row
    down, right = iota((slots, slots), 0), iota((slots, slots), 1)
    rank_row = jnp.sum(jnp.where(same & (down < right), 1, 0), axis=0, keepdims=True)
    rank_col = jnp.sum(jnp.where(same & (right < down), 1, 0), axis=1, keepdims=True)
    spot_col = own_col * 2 + rank_col
    spot_row = jnp.sum(
        jnp.where(slot_ref[...] == iota((slots, rows), 0), spot_col, 0), axis=0, keepdims=True
    )
    sub = iota((HEAD, 128), 0)
    head_ref[...] = jnp.where(sub == 0, id_row, jnp.where(sub == 1, spot_row, 0)).astype(f32)
    peers = atoms_ref.shape[0]
    atom = slot_atom_ref[...] + 1
    mine = iota((peers, slots), 0) == own_row
    first = jnp.sum(jnp.where(mine & (rank_row == 0), atom, 0), axis=1, keepdims=True)
    second = jnp.sum(jnp.where(mine & (rank_row == 1), atom, 0), axis=1, keepdims=True)
    lane = iota((peers, 128), 1)
    atoms = jnp.where(lane == 2 * me, first, jnp.where(lane == 2 * me + 1, second, 0))
    atoms_ref[...] = atoms.astype(f32)


def product_kernel(source_ref, lowered_ref, tiles_ref, head_ref, atoms_ref, out_ref, scratch):
    parts = tiles_ref.shape[0]
    peers = atoms_ref.shape[0]
    rows = parts + 2
    for p in range(parts):
        product = dot(lowered_ref[source_ref[0, p]], tiles_ref[p], 1, 1)
        scratch[pl.ds(p, peers, stride=rows), :] = product
    scratch[pl.ds(parts, peers, stride=rows), :] = jnp.broadcast_to(head_ref[0:1, :], (peers, 128))
    scratch[pl.ds(parts + 1, peers, stride=rows), :] = atoms_ref[...]
    out_ref[...] = scratch[...].astype(bf16)


def combine_kernel(parts, peers, arrived_ref, out_ref, atoms_ref, scratch):
    rows = parts + 2
    targets = out_ref.shape[0]
    scratch[...] = arrived_ref[...].astype(f32)
    heads = scratch[pl.ds(parts, peers, stride=rows), :]
    atoms = jnp.sum(scratch[pl.ds(parts + 1, peers, stride=rows), :], axis=0, keepdims=True)
    atoms_ref[...] = jnp.broadcast_to(atoms, atoms_ref.shape)
    source = iota((peers, 128), 0)
    row = iota((targets, 128), 0).astype(f32)
    chunks = peers * rows // 128
    total = jnp.zeros((targets, 128), f32)
    for r in range(0, chunks, 2):
        hits = []
        for q in range(r, min(r + 2, chunks)):
            item = iota((1, 128), 1) + q * 128
            ids = jnp.sum(jnp.where(source == item // rows, heads, 0.0), axis=0, keepdims=True)
            ids = jnp.where(item % rows < parts, ids + float(OFFSET), -1.0)
            hits.append(jnp.where(row == ids, 1.0, 0.0).astype(bf16))
        items = arrived_ref[r * 128 : (r + len(hits)) * 128, :]
        total = total + dot(jnp.concatenate(hits, axis=1), items, 1, 0)
    out_ref[...] = total.astype(bf16)


def edge_kernel(
    at_ref, columns_ref, up_ref, other_ref, edge_ref, first_ref, second_ref, head_ref, out_ref, send_ref, scratch
):
    narrow = up_ref.shape[0] // len(ORDER)
    triplet = jnp.zeros(out_ref.shape, f32)
    for flip, ref in ((0, up_ref), (STEPS[-1], other_ref)):
        found = []
        for d in ORDER:
            start = pl.multiple_of((at_ref[0] ^ (flip ^ d)) * narrow, narrow)
            found.append(columns_ref[pl.ds(start, narrow), :])
        triplet = triplet + dot(jnp.concatenate(found, axis=0), ref[...], 0, 0)
    joined = (edge_ref[...].astype(f32) + triplet).astype(bf16)
    inner = silu(dot(joined, first_ref[...], 1, 0)).astype(bf16)
    second = silu(dot(inner, second_ref[...], 1, 0))
    update = ((joined.astype(f32) + second) * half_root).astype(bf16)
    out_ref[...] = update
    places = send_ref.shape[0] * 2
    chunks = update.shape[1] // 128
    spot = iota((places, update.shape[0]), 0).astype(f32) == head_ref[1:2, :]
    sums = dot(jnp.where(spot, 1.0, 0.0).astype(bf16), update, 1, 0)
    for c in range(chunks):
        scratch[pl.ds(c, places, stride=chunks), :] = sums[:, c * 128 : (c + 1) * 128]
    send_ref[...] = scratch[...].reshape(send_ref.shape).astype(bf16)


def atom_kernel(arrived_ref, ids_ref, feats_ref, first_ref, second_ref, out_ref, scratch):
    places = arrived_ref.shape[0] * 2
    count, width = feats_ref.shape
    chunks = width // 128
    scratch[...] = arrived_ref[...].astype(f32).reshape(scratch.shape)
    hit = (iota((count, places), 0) + 1).astype(f32) == ids_ref[0:1, :]
    hit = jnp.where(hit, 1.0, 0.0).astype(bf16)
    gathered = jnp.concatenate(
        [
            dot(hit, scratch[pl.ds(c, places, stride=chunks), :].astype(bf16), 1, 0)
            for c in range(chunks)
        ],
        axis=1,
    ).astype(bf16)
    hidden = silu(dot(gathered, first_ref[...], 1, 0)).astype(bf16)
    out_ref[...] = (feats_ref[...].astype(f32) + dot(hidden, second_ref[...], 1, 0)).astype(bf16)


def call(kernel, specs, outs, *args, scratch=(), keep=(), space=pltpu.VMEM):
    args = [
        pltpu.with_memory_space_constraint(a, space) if s is VMEM else a
        for a, s in zip(args, specs)
    ]
    return pl.pallas_call(
        kernel,
        in_specs=specs,
        out_specs=[VMEM] * len(outs),
        out_shape=[
            jax.ShapeDtypeStruct(shape, dtype) if i in keep else pltpu.VMEM(shape, dtype)
            for i, (shape, dtype) in enumerate(outs)
        ],
        scratch_shapes=scratch,
        compiler_params=pltpu.CompilerParams(vmem_limit_bytes=16 << 20),
    )(*args)


def shifted(x, i):
    order = [(j, j ^ STEPS[i]) for j in range(2 * STEPS[0])]
    return lax.ppermute(x, "basis", order)


def body(
    edge_feats,
    pre_weight,
    down_weight,
    angle_tiles,
    part_source,
    part_owner,
    part_target,
    up_weight,
    res_first,
    res_second,
    edge_slot,
    slot_owner,
    slot_atom,
    atom_feats,
    atom_first,
    atom_second,
):
    z_size, blocks = lax.axis_size("z"), lax.axis_size("basis")
    peers = lax.axis_size(GRAPH)
    parts = part_source.shape[0]
    narrow = down_weight.shape[1]
    rows, width = edge_feats.shape
    packed = parts + 2
    near = peers // z_size
    me = lax.axis_index(GRAPH).astype(i32).reshape(1)
    group = lax.axis_index("basis")

    lowered, head, atoms, source = call(
        lambda *refs: lower_kernel((z_size, blocks), *refs), [SMEM] + [VMEM] * 9,
        [((blocks, narrow, rows), bf16), ((HEAD, 128), f32), ((peers, 128), f32), ((1, parts), i32)],
        me, edge_feats, pre_weight, down_weight.T, part_source.reshape(1, parts), part_owner.reshape(1, parts),
        part_target.reshape(1, parts), edge_slot, slot_owner.reshape(1, -1), slot_atom, space=pltpu.HBM,
    )
    lowered, ups = lax.optimization_barrier((lowered, up_weight[0]))
    lowered = lax.all_to_all(lowered, "basis", 0, 0, tiled=True)
    other = shifted(ups, 0)
    at = group.astype(i32).reshape(1)
    (send,) = call(
        product_kernel, [SMEM] + [VMEM] * 4, [((peers * packed, 128), bf16)],
        source, lowered, angle_tiles.reshape(parts, rows, rows), head, atoms,
        scratch=[pltpu.VMEM((peers * packed, 128), f32)],
    )
    arrived = lax.all_to_all(send.reshape(peers, packed // 2, 2, 128), GRAPH, 0, 0, tiled=True)
    ups = jnp.concatenate([ups, other], axis=0)
    ups = jnp.concatenate([ups, shifted(ups, 1)], axis=0)
    other = shifted(ups, 2)
    arrived, at = lax.optimization_barrier((arrived, at))
    summed, ids = call(
        lambda *refs: combine_kernel(parts, peers, *refs), [VMEM],
        [((peers * blocks, 128), bf16), ((HEAD, 128), f32)],
        arrived.reshape(peers * packed, 128),
        scratch=[pltpu.VMEM((peers * packed, 128), f32)],
    )
    far = blocks * z_size
    columns = lax.all_to_all(summed.reshape(near, far, 128), ("x", "core"), 0, 0, tiled=True)
    columns = jnp.swapaxes(columns, 0, 1)
    columns, other = lax.optimization_barrier((columns, other))
    columns = lax.all_to_all(columns, ("basis", "z"), 0, 0, tiled=True)
    edge_update, send = call(
        edge_kernel, [SMEM] + [VMEM] * 7,
        [((rows, width), bf16), ((peers, 2 * width // 128, 128), bf16)],
        at, columns.reshape(peers * blocks, 128), ups, other, edge_feats,
        res_first, res_second, head, keep=(0,),
        scratch=[pltpu.VMEM((peers * 2 * width // 128, 128), f32)],
    )
    arrived = lax.all_to_all(send, GRAPH, 0, 0, tiled=True)
    (atom_update,) = call(
        atom_kernel, [VMEM] * 5, [(atom_feats.shape, bf16)],
        arrived, ids, atom_feats, atom_first, atom_second, keep=(0,),
        scratch=[pltpu.VMEM((peers * 2 * width // 128, 128), f32)],
    )
    return (edge_update, atom_update)


def solution(mesh):
    shape = (mesh.shape["graph"] // 16, 8, 2, mesh.shape["basis"])
    grid = jax.sharding.Mesh(mesh.devices.reshape(shape), GRAPH + ("basis",))
    both = GRAPH + ("basis",)
    in_specs = (
        P(both, None),
        P(),
        P(),
        P(GRAPH, "basis", None, None),
        P(GRAPH),
        P(GRAPH, None),
        P(GRAPH),
        P("basis", None, None),
        P(),
        P(),
        P(both, None),
        P(both, None, None),
        P(both, None),
        P(both, None),
        P(),
        P(),
    )
    out_specs = (P(both, None), P(both, None))
    return jax.shard_map(body, mesh=grid, in_specs=in_specs, out_specs=out_specs, check_vma=False)
```

```python
import jax
import jax.numpy as jnp
from jax import lax
from jax.experimental import pallas as pl
from jax.experimental.pallas import tpu as pltpu
from jax.sharding import PartitionSpec as P

half_root = 0.5**0.5
f32, bf16, i32 = jnp.float32, jnp.bfloat16, jnp.int32
VMEM = pl.BlockSpec(memory_space=pltpu.VMEM)
SMEM = pl.BlockSpec(memory_space=pltpu.SMEM)
GRAPH = ("x", "z", "core")
STEPS = (4, 2, 1)
ORDER = (0, 4, 2, 6)
HEAD = 8
OFFSET = 256


def iota(shape, axis):
    return lax.broadcasted_iota(i32, shape, axis)


def silu(v):
    return v / (1.0 + jnp.exp(-v))


def dot(a, b, left, right):
    return lax.dot_general(a, b, (((left,), (right,)), ((), ())), preferred_element_type=f32)


def lower_kernel(
    sizes, edge_ref, pre_ref, down_ref, source_ref, owner_ref, target_ref, slot_ref, slot_owner_ref,
    slot_atom_ref, out_ref, head_ref, atoms_ref, sources_ref, edges_ref,
):
    edges_ref[...] = edge_ref[...]
    for p in range(source_ref.shape[1]):
        sources_ref[0, p] = source_ref[0, p]
    tables(sizes, owner_ref, target_ref, slot_ref, slot_owner_ref, slot_atom_ref, head_ref, atoms_ref)
    projected = silu(dot(edge_ref[...], pre_ref[...], 1, 0)).astype(bf16)
    lowered = silu(dot(down_ref[...], projected, 1, 1)).astype(bf16)
    for i in range(out_ref.shape[0]):
        out_ref[i] = lowered


def column(row):
    n = row.shape[1]
    return jnp.sum(jnp.where(iota((n, n), 0) == iota((n, n), 1), row, 0), axis=1, keepdims=True)


def tables(sizes, owner_ref, target_ref, slot_ref, slot_owner_ref, slot_atom_ref, head_ref, atoms_ref):
    me = (lax.axis_index("x") * sizes[0] + lax.axis_index("z")) * 2 + lax.axis_index("core")
    parts = owner_ref.shape[1]
    slots = slot_owner_ref.shape[1]
    rows = slot_ref.shape[1]
    owner = column(owner_ref[...])
    z_size, blocks = sizes
    ids = column(target_ref[...]) * (blocks * z_size) + owner - OFFSET
    place = iota((parts, 128), 1) == (iota((parts, 128), 0) + me * (parts + 2)) % 128
    id_row = jnp.sum(jnp.where(place, ids, 0), axis=0, keepdims=True)
    own_row = slot_owner_ref[...]
    own_col = column(own_row)
    same = own_col == own_row
    down, right = iota((slots, slots), 0), iota((slots, slots), 1)
    rank_row = jnp.sum(jnp.where(same & (down < right), 1, 0), axis=0, keepdims=True)
    rank_col = jnp.sum(jnp.where(same & (right < down), 1, 0), axis=1, keepdims=True)
    spot_col = own_col * 2 + rank_col
    spot_row = jnp.sum(
        jnp.where(slot_ref[...] == iota((slots, rows), 0), spot_col, 0), axis=0, keepdims=True
    )
    sub = iota((HEAD, 128), 0)
    head_ref[...] = jnp.where(sub == 0, id_row, jnp.where(sub == 1, spot_row, 0)).astype(f32)
    peers = atoms_ref.shape[0]
    atom = slot_atom_ref[...] + 1
    mine = iota((peers, slots), 0) == own_row
    first = jnp.sum(jnp.where(mine & (rank_row == 0), atom, 0), axis=1, keepdims=True)
    second = jnp.sum(jnp.where(mine & (rank_row == 1), atom, 0), axis=1, keepdims=True)
    lane = iota((peers, 128), 1)
    atoms = jnp.where(lane == 2 * me, first, jnp.where(lane == 2 * me + 1, second, 0))
    atoms_ref[...] = atoms.astype(f32)


def product_kernel(source_ref, lowered_ref, tiles_ref, head_ref, atoms_ref, out_ref, scratch):
    parts = tiles_ref.shape[0]
    peers = atoms_ref.shape[0]
    rows = parts + 2
    for p in range(parts):
        product = dot(lowered_ref[source_ref[0, p]], tiles_ref[p], 1, 1)
        scratch[pl.ds(p, peers, stride=rows), :] = product
    scratch[pl.ds(parts, peers, stride=rows), :] = jnp.broadcast_to(head_ref[0:1, :], (peers, 128))
    scratch[pl.ds(parts + 1, peers, stride=rows), :] = atoms_ref[...]
    out_ref[...] = scratch[...].astype(bf16)


def combine_kernel(parts, peers, arrived_ref, out_ref, atoms_ref, scratch):
    rows = parts + 2
    targets = out_ref.shape[0]
    scratch[...] = arrived_ref[...].astype(f32)
    heads = scratch[pl.ds(parts, peers, stride=rows), :]
    atoms = jnp.sum(scratch[pl.ds(parts + 1, peers, stride=rows), :], axis=0, keepdims=True)
    atoms_ref[...] = jnp.broadcast_to(atoms, atoms_ref.shape)
    source = iota((peers, 128), 0)
    row = iota((targets, 128), 0).astype(f32)
    chunks = peers * rows // 128
    total = jnp.zeros((targets, 128), f32)
    for r in range(0, chunks, 2):
        hits = []
        for q in range(r, min(r + 2, chunks)):
            item = iota((1, 128), 1) + q * 128
            ids = jnp.sum(jnp.where(source == item // rows, heads, 0.0), axis=0, keepdims=True)
            ids = jnp.where(item % rows < parts, ids + float(OFFSET), -1.0)
            hits.append(jnp.where(row == ids, 1.0, 0.0).astype(bf16))
        items = arrived_ref[r * 128 : (r + len(hits)) * 128, :]
        total = total + dot(jnp.concatenate(hits, axis=1), items, 1, 0)
    out_ref[...] = total


def edge_kernel(
    columns_ref, up_ref, other_ref, edge_ref, first_ref, second_ref, head_ref, out_ref, send_ref, scratch
):
    group = lax.axis_index("basis")
    narrow = up_ref.shape[0] // len(ORDER)
    triplet = jnp.zeros(out_ref.shape, f32)
    for flip, ref in ((0, up_ref), (STEPS[-1], other_ref)):
        found = []
        for d in ORDER:
            start = pl.multiple_of((group ^ (flip ^ d)) * narrow, narrow)
            found.append(columns_ref[pl.ds(start, narrow), :])
        triplet = triplet + dot(jnp.concatenate(found, axis=0), ref[...], 0, 0)
    joined = (edge_ref[...].astype(f32) + triplet).astype(bf16)
    inner = silu(dot(joined, first_ref[...], 1, 0)).astype(bf16)
    second = silu(dot(inner, second_ref[...], 1, 0))
    update = ((joined.astype(f32) + second) * half_root).astype(bf16)
    out_ref[...] = update
    places = send_ref.shape[0] * 2
    chunks = update.shape[1] // 128
    spot = iota((places, update.shape[0]), 0).astype(f32) == head_ref[1:2, :]
    sums = dot(jnp.where(spot, 1.0, 0.0).astype(bf16), update, 1, 0)
    for c in range(chunks):
        scratch[pl.ds(c, places, stride=chunks), :] = sums[:, c * 128 : (c + 1) * 128]
    send_ref[...] = scratch[...].reshape(send_ref.shape).astype(bf16)


def atom_kernel(arrived_ref, ids_ref, feats_ref, first_ref, second_ref, out_ref, scratch):
    places = arrived_ref.shape[0] * 2
    count, width = feats_ref.shape
    chunks = width // 128
    scratch[...] = arrived_ref[...].astype(f32).reshape(scratch.shape)
    hit = (iota((count, places), 0) + 1).astype(f32) == ids_ref[0:1, :]
    hit = jnp.where(hit, 1.0, 0.0).astype(bf16)
    gathered = jnp.concatenate(
        [
            dot(hit, scratch[pl.ds(c, places, stride=chunks), :].astype(bf16), 1, 0)
            for c in range(chunks)
        ],
        axis=1,
    ).astype(bf16)
    hidden = silu(dot(gathered, first_ref[...], 1, 0)).astype(bf16)
    out_ref[...] = (feats_ref[...].astype(f32) + dot(hidden, second_ref[...], 1, 0)).astype(bf16)


def call(kernel, specs, outs, *args, scratch=(), keep=(), scalar=(), space=pltpu.VMEM):
    args = [
        pltpu.with_memory_space_constraint(a, space) if s is VMEM or space is pltpu.HBM else a
        for a, s in zip(args, specs)
    ]
    return pl.pallas_call(
        kernel,
        in_specs=specs,
        out_specs=[SMEM if i in scalar else VMEM for i in range(len(outs))],
        out_shape=[
            jax.ShapeDtypeStruct(shape, dtype)
            if i in keep
            else (pltpu.SMEM if i in scalar else pltpu.VMEM)(shape, dtype)
            for i, (shape, dtype) in enumerate(outs)
        ],
        scratch_shapes=scratch,
        compiler_params=pltpu.CompilerParams(vmem_limit_bytes=16 << 20),
    )(*args)


def shifted(x, i):
    order = [(j, j ^ STEPS[i]) for j in range(2 * STEPS[0])]
    return lax.ppermute(x, "basis", order)


def body(
    edge_feats,
    pre_weight,
    down_weight,
    angle_tiles,
    part_source,
    part_owner,
    part_target,
    up_weight,
    res_first,
    res_second,
    edge_slot,
    slot_owner,
    slot_atom,
    atom_feats,
    atom_first,
    atom_second,
):
    z_size, blocks = lax.axis_size("z"), lax.axis_size("basis")
    peers = lax.axis_size(GRAPH)
    parts = part_source.shape[0]
    narrow = down_weight.shape[1]
    rows, width = edge_feats.shape
    packed = parts + 2

    lowered, head, atoms, source, edges = call(
        lambda *refs: lower_kernel((z_size, blocks), *refs), [VMEM] * 3 + [SMEM] + [VMEM] * 5,
        [((blocks, narrow, rows), bf16), ((HEAD, 128), f32), ((peers, 128), f32), ((1, parts), i32), ((rows, width), bf16)],
        edge_feats, pre_weight, down_weight.T, part_source.reshape(1, parts), part_owner.reshape(1, parts),
        part_target.reshape(1, parts), edge_slot, slot_owner.reshape(1, -1), slot_atom, scalar=(3,), space=pltpu.HBM,
    )
    lowered, ups, angle_tiles = lax.optimization_barrier((lowered, up_weight[0], angle_tiles))
    lowered = lax.all_to_all(lowered, "basis", 0, 0, tiled=True)
    other = shifted(ups, 0)
    (send,) = call(
        product_kernel, [SMEM] + [VMEM] * 4, [((peers * packed, 128), bf16)],
        pltpu.with_memory_space_constraint(source, pltpu.SMEM), lowered, angle_tiles.reshape(parts, rows, rows), head, atoms,
        scratch=[pltpu.VMEM((peers * packed, 128), f32)],
    )
    arrived = lax.all_to_all(send.reshape(peers, packed // 2, 2, 128), GRAPH, 0, 0, tiled=True)
    ups = jnp.concatenate([ups, other], axis=0)
    ups = jnp.concatenate([ups, shifted(ups, 1)], axis=0)
    other = shifted(ups, 2)
    summed, ids = call(
        lambda *refs: combine_kernel(parts, peers, *refs), [VMEM],
        [((peers * blocks, 128), f32), ((HEAD, 128), f32)],
        arrived.reshape(peers * packed, 128),
        scratch=[pltpu.VMEM((peers * packed, 128), f32)],
    )
    columns = lax.all_to_all(
        summed.reshape(peers * blocks, 1, 128), ("basis",) + GRAPH, 0, 0, tiled=True
    )
    columns = columns.astype(bf16)
    columns, other = lax.optimization_barrier((columns, other))
    edge_update, send = call(
        edge_kernel, [VMEM] * 7,
        [((rows, width), bf16), ((peers, 2 * width // 128, 128), bf16)],
        columns.reshape(peers * blocks, 128), ups, other, edges,
        res_first, res_second, head, keep=(0,),
        scratch=[pltpu.VMEM((peers * 2 * width // 128, 128), f32)],
    )
    arrived = lax.all_to_all(send, GRAPH, 0, 0, tiled=True)
    (atom_update,) = call(
        atom_kernel, [VMEM] * 5, [(atom_feats.shape, bf16)],
        arrived, ids, atom_feats, atom_first, atom_second, keep=(0,),
        scratch=[pltpu.VMEM((peers * 2 * width // 128, 128), f32)],
    )
    return (edge_update, atom_update)


def solution(mesh):
    shape = (mesh.shape["graph"] // 16, 8, 2, mesh.shape["basis"])
    grid = jax.sharding.Mesh(mesh.devices.reshape(shape), GRAPH + ("basis",))
    both = GRAPH + ("basis",)
    in_specs = (
        P(both, None),
        P(),
        P(),
        P(GRAPH, "basis", None, None),
        P(GRAPH),
        P(GRAPH, None),
        P(GRAPH),
        P("basis", None, None),
        P(),
        P(),
        P(both, None),
        P(both, None, None),
        P(both, None),
        P(both, None),
        P(),
        P(),
    )
    out_specs = (P(both, None), P(both, None))
    return jax.shard_map(body, mesh=grid, in_specs=in_specs, out_specs=out_specs, check_vma=False)
```

```python
import jax
import jax.numpy as jnp
from jax import lax
from jax.experimental import pallas as pl
from jax.experimental.pallas import tpu as pltpu
from jax.sharding import PartitionSpec as P

half_root = 0.5**0.5
f32, bf16, i32 = jnp.float32, jnp.bfloat16, jnp.int32
VMEM = pl.BlockSpec(memory_space=pltpu.VMEM)
SMEM = pl.BlockSpec(memory_space=pltpu.SMEM)
ANY = pl.BlockSpec(memory_space=pl.ANY)
GRAPH = ("x", "z", "core")
STEPS = (4, 2, 1)
ORDER = (0, 4, 2, 6)
SAVES = 4
HEAD = 8
OFFSET = 256


def iota(shape, axis):
    return lax.broadcasted_iota(i32, shape, axis)


def silu(v):
    return v / (1.0 + jnp.exp(-v))


def dot(a, b, left, right):
    return lax.dot_general(a, b, (((left,), (right,)), ((), ())), preferred_element_type=f32)


def lower_kernel(
    sizes, edge_ref, pre_ref, down_ref, source_ref, owner_ref, target_ref, slot_ref, slot_owner_ref,
    slot_atom_ref, out_ref, head_ref, atoms_ref, sources_ref, edges_ref,
):
    edges_ref[...] = edge_ref[...]
    for p in range(source_ref.shape[1]):
        sources_ref[0, p] = source_ref[0, p]
    tables(sizes, owner_ref, target_ref, slot_ref, slot_owner_ref, slot_atom_ref, head_ref, atoms_ref)
    projected = silu(dot(edge_ref[...], pre_ref[...], 1, 0)).astype(bf16)
    lowered = silu(dot(down_ref[...], projected, 1, 1)).astype(bf16)
    for i in range(out_ref.shape[0]):
        out_ref[i] = lowered


def column(row):
    n = row.shape[1]
    return jnp.sum(jnp.where(iota((n, n), 0) == iota((n, n), 1), row, 0), axis=1, keepdims=True)


def tables(sizes, owner_ref, target_ref, slot_ref, slot_owner_ref, slot_atom_ref, head_ref, atoms_ref):
    me = (lax.axis_index("x") * sizes[0] + lax.axis_index("z")) * 2 + lax.axis_index("core")
    parts = owner_ref.shape[1]
    slots = slot_owner_ref.shape[1]
    rows = slot_ref.shape[1]
    owner = column(owner_ref[...])
    z_size, blocks = sizes
    ids = column(target_ref[...]) * (blocks * z_size) + owner - OFFSET
    place = iota((parts, 128), 1) == (iota((parts, 128), 0) + me * (parts + 2)) % 128
    id_row = jnp.sum(jnp.where(place, ids, 0), axis=0, keepdims=True)
    own_row = slot_owner_ref[...]
    own_col = column(own_row)
    same = own_col == own_row
    down, right = iota((slots, slots), 0), iota((slots, slots), 1)
    rank_row = jnp.sum(jnp.where(same & (down < right), 1, 0), axis=0, keepdims=True)
    rank_col = jnp.sum(jnp.where(same & (right < down), 1, 0), axis=1, keepdims=True)
    spot_col = own_col * 2 + rank_col
    spot_row = jnp.sum(
        jnp.where(slot_ref[...] == iota((slots, rows), 0), spot_col, 0), axis=0, keepdims=True
    )
    sub = iota((HEAD, 128), 0)
    head_ref[...] = jnp.where(sub == 0, id_row, jnp.where(sub == 1, spot_row, 0)).astype(f32)
    peers = atoms_ref.shape[0]
    atom = slot_atom_ref[...] + 1
    mine = iota((peers, slots), 0) == own_row
    first = jnp.sum(jnp.where(mine & (rank_row == 0), atom, 0), axis=1, keepdims=True)
    second = jnp.sum(jnp.where(mine & (rank_row == 1), atom, 0), axis=1, keepdims=True)
    lane = iota((peers, 128), 1)
    atoms = jnp.where(lane == 2 * me, first, jnp.where(lane == 2 * me + 1, second, 0))
    atoms_ref[...] = atoms.astype(f32)


def product_kernel(source_ref, lowered_ref, tiles_ref, head_ref, atoms_ref, out_ref, scratch):
    parts = tiles_ref.shape[0]
    peers = atoms_ref.shape[0]
    rows = parts + 2
    for p in range(parts):
        product = dot(lowered_ref[source_ref[0, p]], tiles_ref[p], 1, 1)
        scratch[pl.ds(p, peers, stride=rows), :] = product
    scratch[pl.ds(parts, peers, stride=rows), :] = jnp.broadcast_to(head_ref[0:1, :], (peers, 128))
    scratch[pl.ds(parts + 1, peers, stride=rows), :] = atoms_ref[...]
    out_ref[...] = scratch[...].astype(bf16)


def combine_kernel(parts, peers, arrived_ref, out_ref, atoms_ref, scratch):
    rows = parts + 2
    targets = out_ref.shape[0]
    scratch[...] = arrived_ref[...].astype(f32)
    heads = scratch[pl.ds(parts, peers, stride=rows), :]
    atoms = jnp.sum(scratch[pl.ds(parts + 1, peers, stride=rows), :], axis=0, keepdims=True)
    atoms_ref[...] = jnp.broadcast_to(atoms, atoms_ref.shape)
    source = iota((peers, 128), 0)
    row = iota((targets, 128), 0).astype(f32)
    chunks = peers * rows // 128
    total = jnp.zeros((targets, 128), f32)
    for r in range(0, chunks, 2):
        hits = []
        for q in range(r, min(r + 2, chunks)):
            item = iota((1, 128), 1) + q * 128
            ids = jnp.sum(jnp.where(source == item // rows, heads, 0.0), axis=0, keepdims=True)
            ids = jnp.where(item % rows < parts, ids + float(OFFSET), -1.0)
            hits.append(jnp.where(row == ids, 1.0, 0.0).astype(bf16))
        items = arrived_ref[r * 128 : (r + len(hits)) * 128, :]
        total = total + dot(jnp.concatenate(hits, axis=1), items, 1, 0)
    out_ref[...] = total


def edge_kernel(
    columns_ref, up_ref, other_ref, edge_ref, first_ref, second_ref, head_ref, out_ref, send_ref, scratch
):
    group = lax.axis_index("basis")
    narrow = up_ref.shape[0] // len(ORDER)
    triplet = jnp.zeros(out_ref.shape, f32)
    for flip, ref in ((0, up_ref), (STEPS[-1], other_ref)):
        found = []
        for d in ORDER:
            start = pl.multiple_of((group ^ (flip ^ d)) * narrow, narrow)
            found.append(columns_ref[pl.ds(start, narrow), :])
        triplet = triplet + dot(jnp.concatenate(found, axis=0), ref[...], 0, 0)
    joined = (edge_ref[...].astype(f32) + triplet).astype(bf16)
    inner = silu(dot(joined, first_ref[...], 1, 0)).astype(bf16)
    second = silu(dot(inner, second_ref[...], 1, 0))
    update = ((joined.astype(f32) + second) * half_root).astype(bf16)
    out_ref[...] = update
    places = send_ref.shape[0] * 2
    chunks = update.shape[1] // 128
    spot = iota((places, update.shape[0]), 0).astype(f32) == head_ref[1:2, :]
    sums = dot(jnp.where(spot, 1.0, 0.0).astype(bf16), update, 1, 0)
    for c in range(chunks):
        scratch[pl.ds(c, places, stride=chunks), :] = sums[:, c * 128 : (c + 1) * 128]
    send_ref[...] = scratch[...].reshape(send_ref.shape).astype(bf16)


def atom_kernel(
    arrived_ref, ids_ref, feats_ref, first_ref, second_ref, update_ref, out_ref, saved_ref, scratch, sem
):
    step = update_ref.shape[0] // SAVES
    saves = []
    for i in range(SAVES):
        span = pl.ds(i * step, step)
        saves.append(pltpu.make_async_copy(update_ref.at[span], saved_ref.at[span], sem.at[i]))
        saves[-1].start()
    places = arrived_ref.shape[0] * 2
    count, width = feats_ref.shape
    chunks = width // 128
    scratch[...] = arrived_ref[...].astype(f32).reshape(scratch.shape)
    hit = (iota((count, places), 0) + 1).astype(f32) == ids_ref[0:1, :]
    hit = jnp.where(hit, 1.0, 0.0).astype(bf16)
    gathered = jnp.concatenate(
        [
            dot(hit, scratch[pl.ds(c, places, stride=chunks), :].astype(bf16), 1, 0)
            for c in range(chunks)
        ],
        axis=1,
    ).astype(bf16)
    hidden = silu(dot(gathered, first_ref[...], 1, 0)).astype(bf16)
    out_ref[...] = (feats_ref[...].astype(f32) + dot(hidden, second_ref[...], 1, 0)).astype(bf16)
    for save in saves:
        save.wait()


def call(kernel, specs, outs, *args, scratch=(), keep=(), hand=(), scalar=(), space=pltpu.VMEM):
    args = [
        pltpu.with_memory_space_constraint(a, space) if s is VMEM or space is pltpu.HBM else a
        for a, s in zip(args, specs)
    ]
    return pl.pallas_call(
        kernel,
        in_specs=specs,
        out_specs=[SMEM if i in scalar else ANY if i in hand else VMEM for i in range(len(outs))],
        out_shape=[
            jax.ShapeDtypeStruct(shape, dtype)
            if i in keep + hand
            else (pltpu.SMEM if i in scalar else pltpu.VMEM)(shape, dtype)
            for i, (shape, dtype) in enumerate(outs)
        ],
        scratch_shapes=scratch,
        compiler_params=pltpu.CompilerParams(vmem_limit_bytes=16 << 20),
    )(*args)


def shifted(x, i):
    order = [(j, j ^ STEPS[i]) for j in range(2 * STEPS[0])]
    return lax.ppermute(x, "basis", order)


def body(
    edge_feats,
    pre_weight,
    down_weight,
    angle_tiles,
    part_source,
    part_owner,
    part_target,
    up_weight,
    res_first,
    res_second,
    edge_slot,
    slot_owner,
    slot_atom,
    atom_feats,
    atom_first,
    atom_second,
):
    z_size, blocks = lax.axis_size("z"), lax.axis_size("basis")
    peers = lax.axis_size(GRAPH)
    parts = part_source.shape[0]
    narrow = down_weight.shape[1]
    rows, width = edge_feats.shape
    packed = parts + 2

    lowered, head, atoms, source, edges = call(
        lambda *refs: lower_kernel((z_size, blocks), *refs), [VMEM] * 3 + [SMEM] + [VMEM] * 5,
        [((blocks, narrow, rows), bf16), ((HEAD, 128), f32), ((peers, 128), f32), ((1, parts), i32), ((rows, width), bf16)],
        edge_feats, pre_weight, down_weight.T, part_source.reshape(1, parts), part_owner.reshape(1, parts),
        part_target.reshape(1, parts), edge_slot, slot_owner.reshape(1, -1), slot_atom, scalar=(3,), space=pltpu.HBM,
    )
    lowered, ups, angle_tiles = lax.optimization_barrier((lowered, up_weight[0], angle_tiles))
    lowered = lax.all_to_all(lowered, "basis", 0, 0, tiled=True)
    other = shifted(ups, 0)
    (send,) = call(
        product_kernel, [SMEM] + [VMEM] * 4, [((peers * packed, 128), bf16)],
        pltpu.with_memory_space_constraint(source, pltpu.SMEM), lowered, angle_tiles.reshape(parts, rows, rows), head, atoms,
        scratch=[pltpu.VMEM((peers * packed, 128), f32)],
    )
    arrived = lax.all_to_all(send.reshape(peers, packed // 2, 2, 128), GRAPH, 0, 0, tiled=True)
    ups = jnp.concatenate([ups, other], axis=0)
    ups = jnp.concatenate([ups, shifted(ups, 1)], axis=0)
    other = shifted(ups, 2)
    summed, ids = call(
        lambda *refs: combine_kernel(parts, peers, *refs), [VMEM],
        [((peers * blocks, 128), f32), ((HEAD, 128), f32)],
        arrived.reshape(peers * packed, 128),
        scratch=[pltpu.VMEM((peers * packed, 128), f32)],
    )
    columns = lax.all_to_all(
        summed.reshape(peers * blocks, 1, 128), ("basis",) + GRAPH, 0, 0, tiled=True
    )
    columns = columns.astype(bf16)
    columns, other = lax.optimization_barrier((columns, other))
    edge_update, send = call(
        edge_kernel, [VMEM] * 7,
        [((rows, width), bf16), ((peers, 2 * width // 128, 128), bf16)],
        columns.reshape(peers * blocks, 128), ups, other, edges,
        res_first, res_second, head,
        scratch=[pltpu.VMEM((peers * 2 * width // 128, 128), f32)],
    )
    arrived = lax.all_to_all(send, GRAPH, 0, 0, tiled=True)
    atom_update, edge_update = call(
        atom_kernel, [VMEM] * 6, [(atom_feats.shape, bf16), (edge_update.shape, bf16)],
        arrived, ids, atom_feats, atom_first, atom_second, edge_update, keep=(0,), hand=(1,),
        scratch=[pltpu.VMEM((peers * 2 * width // 128, 128), f32), pltpu.SemaphoreType.DMA((SAVES,))],
    )
    return (edge_update, atom_update)


def solution(mesh):
    shape = (mesh.shape["graph"] // 16, 8, 2, mesh.shape["basis"])
    grid = jax.sharding.Mesh(mesh.devices.reshape(shape), GRAPH + ("basis",))
    both = GRAPH + ("basis",)
    in_specs = (
        P(both, None),
        P(),
        P(),
        P(GRAPH, "basis", None, None),
        P(GRAPH),
        P(GRAPH, None),
        P(GRAPH),
        P("basis", None, None),
        P(),
        P(),
        P(both, None),
        P(both, None, None),
        P(both, None),
        P(both, None),
        P(),
        P(),
    )
    out_specs = (P(both, None), P(both, None))
    return jax.shard_map(body, mesh=grid, in_specs=in_specs, out_specs=out_specs, check_vma=False)
```
